32 devices in a mesh: row: 8 (over z, core), col: 4 (over y, x).
Axes of the slice: x: 2, y: 2, z: 4, core: 2. Of those that a mesh axis runs over, the one named last changes fastest.
Arguments:
- observed: int32 [2048, 32, 1024], P('row', None, 'col'), may hold values 0 or 1
- first_factor: float32 [2048, 256], P(('row', 'col')), may hold values from -1.35 to 1.35
- second_factor: float32 [1024, 256], P(('col', 'row')), may hold values from -1.35 to 1.35
- third_factor: float32 [32, 256], replicated, may hold values from -1.35 to 1.35
Outputs:
- first_out: float32 [2048, 256], P(('row', 'col'))
- second_out: float32 [1024, 256], P(('col', 'row'))
- third_out: float32 [32, 256], replicated
The draws below stay inside these ranges and needn't reach their ends.
All inputs are finite; a program needn't handle non-finite values. No bound on the sum of `observed` on one device may be relied on, other than what follows from the above.
Results may differ from the reference program's by a relative error of at most 0.0003.
Values sent between devices are 32-bit elements; how exact they have to be, the bound alone decides.
No kernel may reach another device: no remote copies, remote signals or barrier semaphores. Data moves between devices by JAX's collectives and lax.ppermute only.
A program may use at most 128 MiB of HBM per device.

```python
import jax
import jax.numpy as jnp
from jax import lax

R = 256
I_DEV = 256
K = 32
STEPS = 2
I = 2048
J = 1024


def drawn_values(key, rows, width):
    values = jax.random.truncated_normal(key, -3.0, 3.0, (rows, width), jnp.float32)
    return jnp.clip(0.45 * values, -1.35, 1.35)


def draw_first_factor(key, part):
    return drawn_values(key, I, R)


def draw_second_factor(key, part):
    return drawn_values(key, J, R)


def draw_third_factor(key, part):
    return drawn_values(key, K, R)


def plant(values, stream_key, smallest, high):
    longest = values.shape.index(max(values.shape))
    spots = []
    for shift in (0, 1):
        where = [jax.random.randint(jax.random.fold_in(stream_key, axis), (), 0, length) for axis, length in enumerate(values.shape)]
        where[longest] = (where[longest] + shift) % values.shape[longest]
        spots.append(tuple(where))
    return values.at[spots[0]].set(smallest).at[spots[1]].set(high)


def setup_inputs(seed: int = 0) -> dict:
    arg_keys = jax.random.split(jax.random.key(seed), 5)
    observed = plant((jax.random.randint(arg_keys[0], (I, K, J), 0, 3) < 1).astype(jnp.int32), jax.random.fold_in(arg_keys[0], 1), 0, 1)
    first_factor = draw_first_factor(jax.random.fold_in(arg_keys[4], 71), 0)
    second_factor = draw_second_factor(jax.random.fold_in(arg_keys[4], 71), 0)
    third_factor = draw_third_factor(jax.random.fold_in(arg_keys[4], 71), 0)
    return {"observed": observed, "first_factor": first_factor, "second_factor": second_factor, "third_factor": third_factor}


step_rate = 48.0
highest = lax.Precision.HIGHEST


def partials(observed_block, rows_block, factor_two, factor_three):
    rows_here, depth_count, cols_here = observed_block.shape
    rank_width = factor_three.shape[1]
    paired = (rows_block[:, None, :] * factor_three[None, :, :]).reshape(rows_here * depth_count, rank_width)
    logits = lax.dot_general(paired, factor_two, (((1,), (1,)), ((), ())), precision=highest, preferred_element_type=jnp.float32)
    derivative = jax.nn.sigmoid(logits) - observed_block.reshape(rows_here * depth_count, cols_here).astype(logits.dtype)
    part_two = lax.dot_general(derivative, paired, (((0,), (0,)), ((), ())), precision=highest, preferred_element_type=jnp.float32)
    carried = jnp.dot(derivative, factor_two, precision=highest, preferred_element_type=jnp.float32)
    carried = carried.reshape(rows_here, depth_count, rank_width)
    part_one = jnp.sum(carried * factor_three[None, :, :], axis=1)
    part_three = jnp.sum(carried * rows_block[:, None, :], axis=0)
    return part_one, part_two, part_three


def reference(observed, first_factor, second_factor, third_factor):
    factor_one, factor_two, factor_three = first_factor, second_factor, third_factor
    for iteration in range(STEPS):
        def accumulate(totals, block_index):
            start = (block_index * I_DEV).astype(jnp.int32)
            rows_block = lax.dynamic_slice_in_dim(factor_one, start, I_DEV, 0)
            observed_block = lax.dynamic_slice_in_dim(observed, start, I_DEV, 0)
            part_one, part_two, part_three = partials(observed_block, rows_block, factor_two, factor_three)
            return (totals[0] + part_two, totals[1] + part_three), part_one

        start_totals = (jnp.zeros((J, R), jnp.float32), jnp.zeros((K, R), jnp.float32))
        blocks = jnp.arange(I // I_DEV, dtype=jnp.int32)
        (grad_two, grad_three), grad_one = lax.scan(accumulate, start_totals, blocks)
        grad_one = grad_one.reshape(I, R)
        factor_one = factor_one - (step_rate / (J * K)) * grad_one
        factor_two = factor_two - (step_rate / (I * K)) * grad_two
        factor_three = factor_three - (step_rate / (I * J)) * grad_three
    return (factor_one, factor_two, factor_three)
```

```python
import functools

import jax
import jax.numpy as jnp
from jax import lax
from jax.experimental import pallas as pl
from jax.experimental.pallas import tpu as pltpu
from jax.sharding import PartitionSpec as P

STEPS = 2
step_rate = 48.0
f32 = jnp.float32
bf16 = jnp.bfloat16


def split(x):
    high = x.astype(bf16)
    low = (x - high.astype(f32)).astype(bf16)
    return high, low


def grad_kernel(obs_ref, a_ref, b_ref, c_ref, ga_ref, gb_ref, gc_ref,
                bt_cat, b_cat, at_cat, gbt, *, depth_block, group):
    g = pl.program_id(0)

    @pl.when(g == 0)
    def _():
        a = a_ref[...]
        b = b_ref[...]
        bh, bl = split(b)
        b_cat[...] = jnp.concatenate([bh, bl, bh], 0)
        bth, btl = split(b.T)
        bt_cat[...] = jnp.concatenate([bth, btl, bth], 0)
        ath, atl = split(a.T)
        at_cat[...] = jnp.concatenate([ath, ath, atl], 1)
        ga_ref[...] = jnp.zeros_like(ga_ref)
        gbt[...] = jnp.zeros_like(gbt)

    a = a_ref[...]
    n = a.shape[0]
    first = pl.multiple_of(g * depth_block, depth_block)
    ck = c_ref[pl.ds(first, depth_block), :]
    ckt = ck.T
    rows_c = []
    for k0 in range(0, depth_block, group):
        wide = []
        for k in range(k0, k0 + group):
            ph, pw = split(a * ck[k:k + 1, :])
            wide.append(jnp.concatenate([ph, ph, pw], 1))
        logits = jnp.dot(jnp.concatenate(wide, 0), bt_cat[...], preferred_element_type=f32)
        x = jnp.concatenate([obs_ref[:, k, :] for k in range(k0, k0 + group)], 0)
        derivative = 0.5 * jnp.tanh(0.5 * logits) + (0.5 - x.astype(f32))
        dh, dw = split(derivative)
        carried = jnp.dot(jnp.concatenate([dh, dh, dw], 1), b_cat[...], preferred_element_type=f32)
        total = None
        for q in range(group):
            k = k0 + q
            cq = carried[q * n:(q + 1) * n]
            term = cq * ck[k:k + 1, :]
            total = term if total is None else total + term
            rows_c.append(jnp.sum(cq * a, axis=0, keepdims=True))
        ga_ref[...] += total
        total = None
        for q in range(group):
            k = k0 + q
            dhq = dh[q * n:(q + 1) * n]
            dwq = dw[q * n:(q + 1) * n]
            gt = jnp.dot(at_cat[...], jnp.concatenate([dhq, dwq, dhq], 0), preferred_element_type=f32)
            term = gt * ckt[:, k:k + 1]
            total = term if total is None else total + term
        gbt[...] += total
    gc_ref[pl.ds(first, depth_block), :] = jnp.concatenate(rows_c, 0)

    @pl.when(g == pl.num_programs(0) - 1)
    def _():
        gb_ref[...] = gbt[...].T


def gradients(observed, a, b, c):
    rows, depth, cols = observed.shape
    rank = a.shape[1]
    depth_block, group = 8, 2
    whole = lambda shape: pl.BlockSpec(shape, lambda g: (0, 0))
    return pl.pallas_call(
        functools.partial(grad_kernel, depth_block=depth_block, group=group),
        grid=(depth // depth_block,),
        in_specs=[
            pl.BlockSpec((rows, depth_block, cols), lambda g: (0, g, 0)),
            whole((rows, rank)), whole((cols, rank)), whole((depth, rank)),
        ],
        out_specs=[whole((rows, rank)), whole((cols, rank)), whole((depth, rank))],
        out_shape=[
            jax.ShapeDtypeStruct((rows, rank), f32),
            jax.ShapeDtypeStruct((cols, rank), f32),
            jax.ShapeDtypeStruct((depth, rank), f32),
        ],
        scratch_shapes=[
            pltpu.VMEM((3 * rank, cols), bf16), pltpu.VMEM((3 * cols, rank), bf16),
            pltpu.VMEM((rank, 3 * rows), bf16), pltpu.VMEM((rank, cols), f32),
        ],
        compiler_params=pltpu.CompilerParams(vmem_limit_bytes=40 * 1024 * 1024),
        cost_estimate=pl.CostEstimate(
            flops=18 * rows * depth * cols * rank, bytes_accessed=4 * rows * depth * cols,
            transcendentals=rows * depth * cols),
    )(observed, a, b, c)


def swap(x, axis, bit):
    n = lax.axis_size(axis)
    return lax.ppermute(x, axis, [(i, i ^ (1 << bit)) for i in range(n)])


def bits_of(axis):
    n = lax.axis_size(axis)
    count = n.bit_length() - 1
    assert n == 1 << count
    return count


def halve(x, axis, bit):
    mine = (lax.axis_index(axis) >> bit) & 1
    place = x.ndim - 3
    keep = lax.dynamic_index_in_dim(x, mine, place, keepdims=False)
    send = lax.dynamic_index_in_dim(x, 1 - mine, place, keepdims=False)
    return keep, send


def join(x, other, axis, bit):
    mine = (lax.axis_index(axis) >> bit) & 1
    place = x.ndim - 2
    low = jnp.where(mine == 0, x, other)
    high = jnp.where(mine == 0, other, x)
    return jnp.stack([low, high], place)


def per_device(observed, first_factor, second_factor, third_factor):
    row_count = lax.axis_size("row")
    col_count = lax.axis_size("col")
    rows_here, depth_count, cols_here = observed.shape
    rank = third_factor.shape[1]
    row_bits = bits_of("row")
    col_bits = bits_of("col")
    rate_one = step_rate / (cols_here * col_count * depth_count)
    rate_two = step_rate / (rows_here * row_count * depth_count)
    rate_three = step_rate / (rows_here * row_count * cols_here * col_count)
    a, b, c = (first_factor, second_factor, third_factor)
    for iteration in range(STEPS):
        wide_a, wide_b = a, b
        for bit in reversed(range(row_bits)):
            wide_b = join(wide_b, swap(wide_b, "row", bit), "row", bit)
        for bit in reversed(range(col_bits)):
            wide_a = join(wide_a, swap(wide_a, "col", bit), "col", bit)
        ga, gb, gc = gradients(
            observed, wide_a.reshape(rows_here, rank), wide_b.reshape(cols_here, rank), c)
        ga = ga.reshape((2,) * col_bits + (-1, rank))
        gb = gb.reshape((2,) * row_bits + (-1, rank))
        for bit in range(max(row_bits, col_bits)):
            if bit < row_bits:
                keep, send = halve(gb, "row", bit)
                gb = keep + swap(send, "row", bit)
                gc = gc + swap(gc, "row", bit)
            if bit < col_bits:
                keep, send = halve(ga, "col", bit)
                ga = keep + swap(send, "col", bit)
                gc = gc + swap(gc, "col", bit)
        a = a - rate_one * ga
        b = b - rate_two * gb
        c = c - rate_three * gc
    return (a, b, c)


def solution(mesh):
    return jax.shard_map(
        per_device,
        mesh=mesh,
        in_specs=(P("row", None, "col"), P(("row", "col"), None), P(("col", "row"), None), P()),
        out_specs=(P(("row", "col"), None), P(("col", "row"), None), P()),
        check_vma=False,
    )
```

```python
import functools

import jax
import jax.numpy as jnp
from jax import lax
from jax.experimental import pallas as pl
from jax.experimental.pallas import tpu as pltpu
from jax.sharding import PartitionSpec as P


STEPS = 2
step_rate = 48.0
f32 = jnp.float32
bf16 = jnp.bfloat16
VMEM_BYTES = 24 * 1024 * 1024


def split(x):
    high = x.astype(bf16)
    low = (x - high.astype(f32)).astype(bf16)
    return high, low


def grad_kernel(obs_hbm, a_ref, b_ref, c_ref, ga_ref, gb_ref, gc_ref,
                obs, bt_cat, b_cat, at_cat, gbt, sems, *, depth_block, group):
    depth = c_ref.shape[0]
    blocks = depth // depth_block
    n, _ = a_ref.shape

    lanes = obs.shape[-1]
    panels = obs.shape[1]

    def fetch(g, h):
        first = pl.multiple_of(g * depth_block, depth_block)
        return pltpu.make_async_copy(
            obs_hbm.at[:, pl.ds(first, depth_block), pl.ds(h * lanes, lanes)],
            obs.at[g, h], sems.at[g, h])

    for g in range(blocks):
        for h in range(panels):
            fetch(g, h).start()
    b = b_ref[...]
    bh, bl = split(b)
    b_cat[...] = jnp.concatenate([bh, bl, bh], 0)
    bth, btl = split(b.T)
    bt_cat[...] = jnp.concatenate([bth, btl, bth], 0)
    ath, atl = split(a_ref[...].T)
    at_cat[...] = jnp.concatenate([ath, ath, atl], 1)
    ga_ref[...] = jnp.zeros_like(ga_ref)
    gbt[...] = jnp.zeros_like(gbt)

    def block(g, carry):
        for h in range(panels):
            fetch(g, h).wait()
        flat = [obs.at[g, h].reshape(n * depth_block, lanes) for h in range(panels)]
        a = a_ref[...]
        first = pl.multiple_of(g * depth_block, depth_block)
        ck = c_ref[pl.ds(first, depth_block), :]
        ckt = ck.T
        rows_c = []
        for k0 in range(0, depth_block, group):
            wide = []
            for k in range(k0, k0 + group):
                ph, pw = split(a * ck[k:k + 1, :])
                wide.append(jnp.concatenate([ph, ph, pw], 1))
            logits = jnp.dot(jnp.concatenate(wide, 0), bt_cat[...], preferred_element_type=f32)
            x = jnp.concatenate([
                jnp.concatenate([p[pl.ds(k, n, stride=depth_block), :] for p in flat], 1)
                for k in range(k0, k0 + group)], 0)
            derivative = 0.5 * jnp.tanh(0.5 * logits) + (0.5 - x.astype(f32))
            dh, dw = split(derivative)
            carried = jnp.dot(
                jnp.concatenate([dh, dh, dw], 1), b_cat[...], preferred_element_type=f32)
            total = None
            for q in range(group):
                k = k0 + q
                cq = carried[q * n:(q + 1) * n]
                term = cq * ck[k:k + 1, :]
                total = term if total is None else total + term
                rows_c.append(jnp.sum(cq * a, axis=0, keepdims=True))
            ga_ref[...] += total
            total = None
            for q in range(group):
                k = k0 + q
                dhq = dh[q * n:(q + 1) * n]
                dwq = dw[q * n:(q + 1) * n]
                gt = jnp.dot(
                    at_cat[...], jnp.concatenate([dhq, dwq, dhq], 0), preferred_element_type=f32)
                term = gt * ckt[:, k:k + 1]
                total = term if total is None else total + term
            gbt[...] += total
        gc_ref[pl.ds(first, depth_block), :] = jnp.concatenate(rows_c, 0)
        return carry

    lax.fori_loop(0, blocks, block, 0)
    gb_ref[...] = gbt[...].T


def gradients(observed, a, b, c):
    rows, depth, cols = observed.shape
    rank = a.shape[1]
    depth_block, group, lanes = 8, 2, 128
    here = pl.BlockSpec(memory_space=pltpu.VMEM)
    return pl.pallas_call(
        functools.partial(grad_kernel, depth_block=depth_block, group=group),
        in_specs=[pl.BlockSpec(memory_space=pltpu.HBM), here, here, here],
        out_specs=[here, here, here],
        out_shape=[
            jax.ShapeDtypeStruct((rows, rank), f32),
            jax.ShapeDtypeStruct((cols, rank), f32),
            jax.ShapeDtypeStruct((depth, rank), f32),
        ],
        scratch_shapes=[
            pltpu.VMEM((depth // depth_block, cols // lanes, rows, depth_block, lanes), jnp.int32),
            pltpu.VMEM((3 * rank, cols), bf16), pltpu.VMEM((3 * cols, rank), bf16),
            pltpu.VMEM((rank, 3 * rows), bf16), pltpu.VMEM((rank, cols), f32),
            pltpu.SemaphoreType.DMA((depth // depth_block, cols // lanes)),
        ],
        compiler_params=pltpu.CompilerParams(vmem_limit_bytes=VMEM_BYTES),
        cost_estimate=pl.CostEstimate(
            flops=18 * rows * depth * cols * rank, bytes_accessed=4 * rows * depth * cols,
            transcendentals=rows * depth * cols),
    )(pltpu.with_memory_space_constraint(observed, pltpu.HBM), a, b, c)


def exchange(x, axis, mask):
    n = lax.axis_size(axis)
    return lax.ppermute(x, axis, [(i, i ^ mask) for i in range(n)])


def stage_kernel(a_hbm, b_hbm, c_hbm, a_ref, b_ref, c_ref, sems):
    copies = [
        pltpu.make_async_copy(src, dst, sems.at[i])
        for i, (src, dst) in enumerate(((a_hbm, a_ref), (b_hbm, b_ref), (c_hbm, c_ref)))
    ]
    for copy in copies:
        copy.start()
    for copy in copies:
        copy.wait()


def staged(a, b, c):
    return pl.pallas_call(
        stage_kernel,
        in_specs=[pl.BlockSpec(memory_space=pltpu.HBM)] * 3,
        out_specs=[pl.BlockSpec(memory_space=pltpu.VMEM)] * 3,
        out_shape=[jax.ShapeDtypeStruct(x.shape, x.dtype) for x in (a, b, c)],
        scratch_shapes=[pltpu.SemaphoreType.DMA((3,))],
        compiler_params=pltpu.CompilerParams(vmem_limit_bytes=VMEM_BYTES),
    )(*[pltpu.with_memory_space_constraint(x, pltpu.HBM) for x in (a, b, c)])


def tree_sum(terms):
    while len(terms) > 1:
        terms = [terms[i] + terms[i + 1] for i in range(0, len(terms), 2)]
    return terms[0]


def take(x, index):
    return lax.dynamic_index_in_dim(x, index, 0, keepdims=False)


def in_order(parts, index):
    x = jnp.stack(parts)
    n = x.shape[0]
    width = 1
    while width < n:
        y = x.reshape((n // (2 * width), 2, width) + x.shape[1:])
        flipped = jnp.stack([y[:, 1], y[:, 0]], 1)
        x = jnp.where((index & width) != 0, flipped, y).reshape(x.shape)
        width *= 2
    return x


def per_device(observed, first_factor, second_factor, third_factor):
    row_count = lax.axis_size("row")
    col_count = lax.axis_size("col")
    chip_count = row_count // 2
    for n in (chip_count, col_count):
        assert n & (n - 1) == 0
    rows_here, depth_count, cols_here = observed.shape
    rank = third_factor.shape[1]
    rows_own, cols_own = first_factor.shape[0], second_factor.shape[0]
    half_depth = depth_count // 2
    cols_half = cols_here // 2
    row = lax.axis_index("row")
    col = lax.axis_index("col")
    core, chip = row & 1, row >> 1
    rate_one = step_rate / (cols_here * col_count * depth_count)
    rate_two = step_rate / (rows_here * row_count * depth_count)
    rate_three = step_rate / (rows_here * row_count * cols_here * col_count)
    chip_masks = []
    bit = 1
    while bit < chip_count:
        chip_masks.append(bit | (bit >> 1))
        bit *= 2

    def gather_rows(own, sent):
        parts = [own] + [exchange(sent, "col", s) for s in range(1, col_count)]
        return in_order(parts, col).reshape(rows_here, rank)

    def both_cores(half, depth_half):
        other = exchange(jnp.concatenate([half.reshape(cols_half, rank), depth_half]), "row", 1)
        other_half = other[:cols_half].reshape(half.shape)
        other_depth = other[cols_half:]
        wide = jnp.where(core == 0, jnp.stack([half, other_half], 1), jnp.stack([other_half, half], 1))
        depth = jnp.where(core == 0, jnp.concatenate([depth_half, other_depth]),
                          jnp.concatenate([other_depth, depth_half]))
        return wide.reshape(cols_here, rank), depth

    a, b, c = staged(first_factor, second_factor, third_factor)
    c_half = lax.dynamic_slice_in_dim(c, core * half_depth, half_depth, 0)
    held = [b]
    places = [0]
    mask = chip_count // 2
    while mask:
        sent = jnp.stack(held) if len(held) > 1 else second_factor[None]
        got = exchange(sent, "row", 2 * mask)
        held = held + [got[i] for i in range(len(held))]
        places = places + [p ^ mask for p in places]
        mask //= 2
    b_half = in_order([held[places.index(s)] for s in range(chip_count)], chip)
    wide_a = gather_rows(a, first_factor)
    wide_b, c = both_cores(b_half, c_half)
    for iteration in range(STEPS):
        last = iteration == STEPS - 1
        ga, gb, gc = gradients(observed, wide_a, wide_b, c)
        ga = ga.reshape(col_count, rows_own, rank)
        gb = gb.reshape(chip_count, 2, cols_own, rank)
        gc = gc.reshape(2, half_depth, rank)
        pick = lambda x, axis, which: lax.dynamic_index_in_dim(x, which, axis, keepdims=False)
        got = exchange(
            jnp.concatenate([pick(gb, 1, 1 - core).reshape(cols_half, rank), pick(gc, 0, 1 - core)]), "row", 1)
        gb = pick(gb, 1, core) + got[:cols_half].reshape(chip_count, cols_own, rank)
        gc = pick(gc, 0, core) + got[cols_half:]
        parts = [jnp.concatenate([take(ga, col), gc])]
        for s in range(1, col_count):
            parts.append(exchange(jnp.concatenate([take(ga, col ^ s), gc]), "col", s))
        both = tree_sum(parts)
        a = a - rate_one * both[:rows_own]
        gc = both[rows_own:]
        if last:
            parts = [jnp.concatenate([take(gb, chip), gc])]
            for s in range(1, chip_count):
                parts.append(exchange(jnp.concatenate([take(gb, chip ^ s), gc]), "row", 2 * s))
            both = tree_sum(parts)
            b = take(b_half, chip) - rate_two * both[:cols_own]
            c_half = c_half - rate_three * both[cols_own:]
            other = exchange(c_half, "row", 1)
            c = jnp.where(core == 0, jnp.concatenate([c_half, other]), jnp.concatenate([other, c_half]))
        else:
            both = jnp.concatenate([gb.reshape(cols_half, rank), gc])
            for mask in chip_masks:
                both = both + exchange(both, "row", 2 * mask)
            wide_a = gather_rows(a, a)
            b_half = b_half - rate_two * both[:cols_half].reshape(b_half.shape)
            c_half = c_half - rate_three * both[cols_half:]
            wide_b, c = both_cores(b_half, c_half)
    return (a, b, c)


def solution(mesh):
    return jax.shard_map(
        per_device,
        mesh=mesh,
        in_specs=(P("row", None, "col"), P(("row", "col"), None), P(("col", "row"), None), P()),
        out_specs=(P(("row", "col"), None), P(("col", "row"), None), P()),
        check_vma=False,
    )
```

```python
import functools

import jax
import jax.numpy as jnp
from jax import lax
from jax.experimental import pallas as pl
from jax.experimental.pallas import tpu as pltpu
from jax.sharding import PartitionSpec as P


STEPS = 2
step_rate = 48.0
f32 = jnp.float32
bf16 = jnp.bfloat16
VMEM_BYTES = 20 * 1024 * 1024


def split(x):
    high = x.astype(bf16)
    low = (x - high.astype(f32)).astype(bf16)
    return high, low


def panel_copy(obs_hbm, dst, sem, block, panel, depth_block):
    lanes = dst.shape[-1]
    return pltpu.make_async_copy(
        obs_hbm.at[:, pl.ds(block * depth_block, depth_block), pl.ds(panel * lanes, lanes)], dst, sem)


def grad_kernel(obs_hbm, head_ref, a_ref, b_ref, c_ref, ga_ref, keep_ref, send_ref,
                obs, bt_cat, b_cat, at_cat, gbt, gb_ref, gc_ref, sems, *, group, cols_own):
    panels, n, depth_block, lanes = head_ref.shape
    blocks = c_ref.shape[0] // depth_block

    def fetch(g, h):
        return panel_copy(obs_hbm, obs.at[g, h], sems.at[g, h], g + 1, h, depth_block)

    for g in range(blocks - 1):
        for h in range(panels):
            fetch(g, h).start()
    b = b_ref[...]
    bh, bl = split(b)
    b_cat[...] = jnp.concatenate([bh, bl, bh], 0)
    bth, btl = split(b.T)
    bt_cat[...] = jnp.concatenate([bth, btl, bth], 0)
    ath, atl = split(a_ref[...].T)
    at_cat[...] = jnp.concatenate([ath, ath, atl], 1)
    ga_ref[...] = jnp.zeros_like(ga_ref)
    gbt[...] = jnp.zeros_like(gbt)

    def block(g, source):
        flat = [source.at[h].reshape(n * depth_block, lanes) for h in range(panels)]
        a = a_ref[...]
        base = pl.multiple_of(g * depth_block, depth_block)
        ck = c_ref[pl.ds(base, depth_block), :]
        ckt = ck.T
        rows_c = []

        def front(k0):
            wide = []
            for k in range(k0, k0 + group):
                ph, pw = split(a * ck[k:k + 1, :])
                wide.append(jnp.concatenate([ph, ph, pw], 1))
            return jnp.dot(jnp.concatenate(wide, 0), bt_cat[...], preferred_element_type=f32)

        later = front(0)
        for k0 in range(0, depth_block, group):
            logits = later
            if k0 + group < depth_block:
                later = front(k0 + group)
            x = jnp.concatenate([
                jnp.concatenate([p[pl.ds(k, n, stride=depth_block), :] for p in flat], 1)
                for k in range(k0, k0 + group)], 0)
            derivative = 0.5 * jnp.tanh(0.5 * logits) + (0.5 - x.astype(f32))
            dh, dw = split(derivative)
            carried = jnp.dot(
                jnp.concatenate([dh, dh, dw], 1), b_cat[...], preferred_element_type=f32)
            total = None
            for q in range(group):
                k = k0 + q
                cq = carried[q * n:(q + 1) * n]
                term = cq * ck[k:k + 1, :]
                total = term if total is None else total + term
                rows_c.append(jnp.sum(cq * a, axis=0, keepdims=True))
            ga_ref[...] += total
            total = None
            for q in range(group):
                k = k0 + q
                dhq = dh[q * n:(q + 1) * n]
                dwq = dw[q * n:(q + 1) * n]
                gt = jnp.dot(
                    at_cat[...], jnp.concatenate([dhq, dwq, dhq], 0), preferred_element_type=f32)
                term = gt * ckt[:, k:k + 1]
                total = term if total is None else total + term
            gbt[...] += total
        gc_ref[pl.ds(base, depth_block), :] = jnp.concatenate(rows_c, 0)

    block(0, head_ref)

    def rest(g, carry):
        for h in range(panels):
            fetch(g, h).wait()
        block(g + 1, obs.at[g])
        return carry

    lax.fori_loop(0, blocks - 1, rest, 0)
    gb_ref[...] = gbt[...].T
    core = lax.axis_index("row") & 1
    half_depth = gc_ref.shape[0] // 2
    half = gb_ref.shape[0] // 2
    for ref, which in ((keep_ref, core), (send_ref, 1 - core)):
        for p in range(half // cols_own):
            start = pl.multiple_of((2 * p + which) * cols_own, cols_own)
            ref[p * cols_own:(p + 1) * cols_own, :] = gb_ref[pl.ds(start, cols_own), :]
        start = pl.multiple_of(which * half_depth, half_depth)
        ref[half:, :] = gc_ref[pl.ds(start, half_depth), :]


def gradients(observed, head, a, b, c, cols_own):
    rows, depth, cols = observed.shape
    rank = a.shape[1]
    panels, _, depth_block, lanes = head.shape
    blocks = depth // depth_block
    here = pl.BlockSpec(memory_space=pltpu.VMEM)
    return pl.pallas_call(
        functools.partial(grad_kernel, group=2, cols_own=cols_own),
        in_specs=[pl.BlockSpec(memory_space=pltpu.HBM), here, here, here, here],
        out_specs=[here, here, here],
        out_shape=[
            jax.ShapeDtypeStruct((rows, rank), f32),
            jax.ShapeDtypeStruct(((cols + depth) // 2, rank), f32),
            jax.ShapeDtypeStruct(((cols + depth) // 2, rank), f32),
        ],
        scratch_shapes=[
            pltpu.VMEM((blocks - 1, panels, rows, depth_block, lanes), jnp.int32),
            pltpu.VMEM((3 * rank, cols), bf16), pltpu.VMEM((3 * cols, rank), bf16),
            pltpu.VMEM((rank, 3 * rows), bf16), pltpu.VMEM((rank, cols), f32),
            pltpu.VMEM((cols, rank), f32), pltpu.VMEM((depth, rank), f32),
            pltpu.SemaphoreType.DMA((blocks - 1, panels)),
        ],
        compiler_params=pltpu.CompilerParams(vmem_limit_bytes=VMEM_BYTES),
        cost_estimate=pl.CostEstimate(
            flops=18 * rows * depth * cols * rank, bytes_accessed=4 * rows * depth * cols,
            transcendentals=rows * depth * cols),
    )(pltpu.with_memory_space_constraint(observed, pltpu.HBM), head, a, b, c)


def head_kernel(obs_hbm, head_ref, sems):
    copies = [
        panel_copy(obs_hbm, head_ref.at[h], sems.at[h], 0, h, head_ref.shape[2])
        for h in range(head_ref.shape[0])
    ]
    for copy in copies:
        copy.start()
    for copy in copies:
        copy.wait()


def first_block(observed, depth_block, lanes):
    rows, _, cols = observed.shape
    panels = cols // lanes
    return pl.pallas_call(
        head_kernel,
        in_specs=[pl.BlockSpec(memory_space=pltpu.HBM)],
        out_specs=pl.BlockSpec(memory_space=pltpu.VMEM),
        out_shape=jax.ShapeDtypeStruct((panels, rows, depth_block, lanes), observed.dtype),
        scratch_shapes=[pltpu.SemaphoreType.DMA((panels,))],
        compiler_params=pltpu.CompilerParams(vmem_limit_bytes=VMEM_BYTES),
    )(pltpu.with_memory_space_constraint(observed, pltpu.HBM))


def exchange(x, axis, mask):
    n = lax.axis_size(axis)
    return lax.ppermute(x, axis, [(i, i ^ mask) for i in range(n)])


def stage_kernel(a_hbm, b_hbm, c_hbm, a_ref, b_ref, c_ref, sems):
    copies = [
        pltpu.make_async_copy(src, dst, sems.at[i])
        for i, (src, dst) in enumerate(((a_hbm, a_ref), (b_hbm, b_ref), (c_hbm, c_ref)))
    ]
    for copy in copies:
        copy.start()
    for copy in copies:
        copy.wait()


def staged(a, b, c):
    return pl.pallas_call(
        stage_kernel,
        in_specs=[pl.BlockSpec(memory_space=pltpu.HBM)] * 3,
        out_specs=[pl.BlockSpec(memory_space=pltpu.VMEM)] * 3,
        out_shape=[jax.ShapeDtypeStruct(x.shape, x.dtype) for x in (a, b, c)],
        scratch_shapes=[pltpu.SemaphoreType.DMA((3,))],
        compiler_params=pltpu.CompilerParams(vmem_limit_bytes=VMEM_BYTES),
    )(*[pltpu.with_memory_space_constraint(x, pltpu.HBM) for x in (a, b, c)])


def tree_sum(terms):
    while len(terms) > 1:
        terms = [terms[i] + terms[i + 1] for i in range(0, len(terms), 2)]
    return terms[0]


def take(x, index):
    return lax.dynamic_index_in_dim(x, index, 0, keepdims=False)


def in_order(parts, index):
    x = jnp.stack(parts)
    n = x.shape[0]
    width = 1
    while width < n:
        y = x.reshape((n // (2 * width), 2, width) + x.shape[1:])
        flipped = jnp.stack([y[:, 1], y[:, 0]], 1)
        x = jnp.where((index & width) != 0, flipped, y).reshape(x.shape)
        width *= 2
    return x


def per_device(observed, first_factor, second_factor, third_factor):
    row_count = lax.axis_size("row")
    col_count = lax.axis_size("col")
    chip_count = row_count // 2
    for n in (chip_count, col_count):
        assert n & (n - 1) == 0
    rows_here, depth_count, cols_here = observed.shape
    rank = third_factor.shape[1]
    rows_own, cols_own = first_factor.shape[0], second_factor.shape[0]
    half_depth = depth_count // 2
    cols_half = cols_here // 2
    row = lax.axis_index("row")
    col = lax.axis_index("col")
    core, chip = row & 1, row >> 1
    rate_one = step_rate / (cols_here * col_count * depth_count)
    rate_two = step_rate / (rows_here * row_count * depth_count)
    rate_three = step_rate / (rows_here * row_count * cols_here * col_count)
    chip_masks = []
    bit = 1
    while bit < chip_count:
        chip_masks.append(bit | (bit >> 1))
        bit *= 2

    def gather_rows(own, sent):
        parts = [own] + [exchange(sent, "col", s) for s in range(1, col_count)]
        return in_order(parts, col).reshape(rows_here, rank)

    def both_cores(half, depth_half):
        other = exchange(jnp.concatenate([half.reshape(cols_half, rank), depth_half]), "row", 1)
        other_half = other[:cols_half].reshape(half.shape)
        other_depth = other[cols_half:]
        wide = jnp.where(core == 0, jnp.stack([half, other_half], 1), jnp.stack([other_half, half], 1))
        depth = jnp.where(core == 0, jnp.concatenate([depth_half, other_depth]),
                          jnp.concatenate([other_depth, depth_half]))
        return wide.reshape(cols_here, rank), depth

    a, b, c = staged(first_factor, second_factor, third_factor)
    head = first_block(observed, 8, 128)
    c_half = lax.dynamic_slice_in_dim(c, core * half_depth, half_depth, 0)
    held = [b]
    places = [0]
    mask = chip_count // 2
    while mask:
        sent = jnp.stack(held) if len(held) > 1 else second_factor[None]
        got = exchange(sent, "row", 2 * mask)
        held = held + [got[i] for i in range(len(held))]
        places = places + [p ^ mask for p in places]
        mask //= 2
    b_half = in_order([held[places.index(s)] for s in range(chip_count)], chip)
    wide_a = gather_rows(a, first_factor)
    wide_b, c = both_cores(b_half, c_half)
    for iteration in range(STEPS):
        last = iteration == STEPS - 1
        ga, keep, send = gradients(observed, head, wide_a, wide_b, c, cols_own)
        ga = ga.reshape(col_count, rows_own, rank)
        both = keep + exchange(send, "row", 1)
        gb, gc = both[:cols_half], both[cols_half:]
        parts = [jnp.concatenate([take(ga, col), gc])]
        for s in range(1, col_count):
            parts.append(exchange(jnp.concatenate([take(ga, col ^ s), gc]), "col", s))
        both = tree_sum(parts)
        a = a - rate_one * both[:rows_own]
        gc = both[rows_own:]
        if last:
            gb = gb.reshape(chip_count, cols_own, rank)
            parts = [jnp.concatenate([take(gb, chip), gc])]
            for s in range(1, chip_count):
                parts.append(exchange(jnp.concatenate([take(gb, chip ^ s), gc]), "row", 2 * s))
            both = tree_sum(parts)
            b = take(b_half, chip) - rate_two * both[:cols_own]
            c_half = c_half - rate_three * both[cols_own:]
            other = exchange(c_half, "row", 1)
            c = jnp.where(core == 0, jnp.concatenate([c_half, other]), jnp.concatenate([other, c_half]))
        else:
            both = jnp.concatenate([gb, gc])
            for mask in chip_masks:
                both = both + exchange(both, "row", 2 * mask)
            wide_a = gather_rows(a, a)
            b_half = b_half - rate_two * both[:cols_half].reshape(b_half.shape)
            c_half = c_half - rate_three * both[cols_half:]
            wide_b, c = both_cores(b_half, c_half)
    return (a, b, c)


def solution(mesh):
    return jax.shard_map(
        per_device,
        mesh=mesh,
        in_specs=(P("row", None, "col"), P(("row", "col"), None), P(("col", "row"), None), P()),
        out_specs=(P(("row", "col"), None), P(("col", "row"), None), P()),
        check_vma=False,
    )
```

```python
import functools

import jax
import jax.numpy as jnp
from jax import lax
from jax.experimental import pallas as pl
from jax.experimental.pallas import tpu as pltpu
from jax.sharding import PartitionSpec as P


STEPS = 2
step_rate = 48.0
f32 = jnp.float32
bf16 = jnp.bfloat16
VMEM_BYTES = 20 * 1024 * 1024


def split(x):
    high = x.astype(bf16)
    low = (x - high.astype(f32)).astype(bf16)
    return high, low


def panel_copy(obs_hbm, dst, sem, block, panel, depth_block):
    lanes = dst.shape[-1]
    return pltpu.make_async_copy(
        obs_hbm.at[:, pl.ds(block * depth_block, depth_block), pl.ds(panel * lanes, lanes)], dst, sem)


def grad_kernel(obs_hbm, head_ref, a_ref, b_ref, c_ref, ga_ref, keep_ref, send_ref,
                obs, bt_cat, b_cat, at_cat, gbt, gb_ref, gc_ref, ahead, sems, *, group, cols_own):
    panels, n, depth_block, lanes = head_ref.shape
    blocks = c_ref.shape[0] // depth_block

    def fetch(g, h):
        return panel_copy(obs_hbm, obs.at[g, h], sems.at[g, h], g + 1, h, depth_block)

    for g in range(blocks - 1):
        for h in range(panels):
            fetch(g, h).start()
    b = b_ref[...]
    bh, bl = split(b)
    b_cat[...] = jnp.concatenate([bh, bl, bh], 0)
    bth, btl = split(b.T)
    bt_cat[...] = jnp.concatenate([bth, btl, bth], 0)
    ath, atl = split(a_ref[...].T)
    at_cat[...] = jnp.concatenate([ath, ath, atl], 1)
    ga_ref[...] = jnp.zeros_like(ga_ref)
    gbt[...] = jnp.zeros_like(gbt)

    def front(rows):
        wide = []
        for k in range(group):
            ph, pw = split(a_ref[...] * rows[k:k + 1, :])
            wide.append(jnp.concatenate([ph, ph, pw], 1))
        return jnp.dot(jnp.concatenate(wide, 0), bt_cat[...], preferred_element_type=f32)

    def block(g, source, more=True):
        flat = [source.at[h].reshape(n * depth_block, lanes) for h in range(panels)]
        a = a_ref[...]
        base = pl.multiple_of(g * depth_block, depth_block)
        ck = c_ref[pl.ds(base, depth_block), :]
        ckt = ck.T
        rows_c = []

        if more:
            following = c_ref[pl.ds(pl.multiple_of(base + depth_block, depth_block), depth_block), :]
        later = ahead[...]
        for k0 in range(0, depth_block, group):
            logits = later
            if k0 + group < depth_block:
                later = front(ck[k0 + group:k0 + 2 * group])
            elif more:
                ahead[...] = front(following[:group])
            x = jnp.concatenate([
                jnp.concatenate([p[pl.ds(k, n, stride=depth_block), :] for p in flat], 1)
                for k in range(k0, k0 + group)], 0)
            derivative = 0.5 * jnp.tanh(0.5 * logits) + (0.5 - x.astype(f32))
            dh, dw = split(derivative)
            carried = jnp.dot(
                jnp.concatenate([dh, dh, dw], 1), b_cat[...], preferred_element_type=f32)
            total = None
            for q in range(group):
                k = k0 + q
                cq = carried[q * n:(q + 1) * n]
                term = cq * ck[k:k + 1, :]
                total = term if total is None else total + term
                rows_c.append(jnp.sum(cq * a, axis=0, keepdims=True))
            ga_ref[...] += total
            total = None
            for q in range(group):
                k = k0 + q
                dhq = dh[q * n:(q + 1) * n]
                dwq = dw[q * n:(q + 1) * n]
                gt = jnp.dot(
                    at_cat[...], jnp.concatenate([dhq, dwq, dhq], 0), preferred_element_type=f32)
                term = gt * ckt[:, k:k + 1]
                total = term if total is None else total + term
            gbt[...] += total
        gc_ref[pl.ds(base, depth_block), :] = jnp.concatenate(rows_c, 0)

    def rest(g, carry):
        for h in range(panels):
            fetch(g, h).wait()
        block(g + 1, obs.at[g])
        return carry

    ahead[...] = front(c_ref[:group, :])
    block(0, head_ref)
    lax.fori_loop(0, blocks - 2, rest, 0)
    for h in range(panels):
        fetch(blocks - 2, h).wait()
    block(blocks - 1, obs.at[blocks - 2], more=False)
    gb_ref[...] = gbt[...].T
    core = lax.axis_index("row") & 1
    half_depth = gc_ref.shape[0] // 2
    half = gb_ref.shape[0] // 2
    for ref, which in ((keep_ref, core), (send_ref, 1 - core)):
        for p in range(half // cols_own):
            start = pl.multiple_of((2 * p + which) * cols_own, cols_own)
            ref[p * cols_own:(p + 1) * cols_own, :] = gb_ref[pl.ds(start, cols_own), :]
        start = pl.multiple_of(which * half_depth, half_depth)
        ref[half:, :] = gc_ref[pl.ds(start, half_depth), :]


def gradients(observed, head, a, b, c, cols_own):
    rows, depth, cols = observed.shape
    rank = a.shape[1]
    panels, _, depth_block, lanes = head.shape
    blocks = depth // depth_block
    group = 1
    here = pl.BlockSpec(memory_space=pltpu.VMEM)
    return pl.pallas_call(
        functools.partial(grad_kernel, group=group, cols_own=cols_own),
        in_specs=[pl.BlockSpec(memory_space=pltpu.HBM), here, here, here, here],
        out_specs=[here, here, here],
        out_shape=[
            jax.ShapeDtypeStruct((rows, rank), f32),
            jax.ShapeDtypeStruct(((cols + depth) // 2, rank), f32),
            jax.ShapeDtypeStruct(((cols + depth) // 2, rank), f32),
        ],
        scratch_shapes=[
            pltpu.VMEM((blocks - 1, panels, rows, depth_block, lanes), jnp.int32),
            pltpu.VMEM((3 * rank, cols), bf16), pltpu.VMEM((3 * cols, rank), bf16),
            pltpu.VMEM((rank, 3 * rows), bf16), pltpu.VMEM((rank, cols), f32),
            pltpu.VMEM((cols, rank), f32), pltpu.VMEM((depth, rank), f32),
            pltpu.VMEM((group * rows, cols), f32),
            pltpu.SemaphoreType.DMA((blocks - 1, panels)),
        ],
        compiler_params=pltpu.CompilerParams(vmem_limit_bytes=VMEM_BYTES),
        cost_estimate=pl.CostEstimate(
            flops=18 * rows * depth * cols * rank, bytes_accessed=4 * rows * depth * cols,
            transcendentals=rows * depth * cols),
    )(pltpu.with_memory_space_constraint(observed, pltpu.HBM), head, a, b, c)


def head_kernel(obs_hbm, head_ref, sems):
    copies = [
        panel_copy(obs_hbm, head_ref.at[h], sems.at[h], 0, h, head_ref.shape[2])
        for h in range(head_ref.shape[0])
    ]
    for copy in copies:
        copy.start()
    for copy in copies:
        copy.wait()


def first_block(observed, depth_block, lanes):
    rows, _, cols = observed.shape
    panels = cols // lanes
    return pl.pallas_call(
        head_kernel,
        in_specs=[pl.BlockSpec(memory_space=pltpu.HBM)],
        out_specs=pl.BlockSpec(memory_space=pltpu.VMEM),
        out_shape=jax.ShapeDtypeStruct((panels, rows, depth_block, lanes), observed.dtype),
        scratch_shapes=[pltpu.SemaphoreType.DMA((panels,))],
        compiler_params=pltpu.CompilerParams(vmem_limit_bytes=VMEM_BYTES),
    )(pltpu.with_memory_space_constraint(observed, pltpu.HBM))


def exchange(x, axis, mask):
    n = lax.axis_size(axis)
    return lax.ppermute(x, axis, [(i, i ^ mask) for i in range(n)])


def stage_kernel(a_hbm, b_hbm, c_hbm, a_ref, b_ref, c_ref, sems):
    copies = [
        pltpu.make_async_copy(src, dst, sems.at[i])
        for i, (src, dst) in enumerate(((a_hbm, a_ref), (b_hbm, b_ref), (c_hbm, c_ref)))
    ]
    for copy in copies:
        copy.start()
    for copy in copies:
        copy.wait()


def staged(a, b, c):
    return pl.pallas_call(
        stage_kernel,
        in_specs=[pl.BlockSpec(memory_space=pltpu.HBM)] * 3,
        out_specs=[pl.BlockSpec(memory_space=pltpu.VMEM)] * 3,
        out_shape=[jax.ShapeDtypeStruct(x.shape, x.dtype) for x in (a, b, c)],
        scratch_shapes=[pltpu.SemaphoreType.DMA((3,))],
        compiler_params=pltpu.CompilerParams(vmem_limit_bytes=VMEM_BYTES),
    )(*[pltpu.with_memory_space_constraint(x, pltpu.HBM) for x in (a, b, c)])


def tree_sum(terms):
    while len(terms) > 1:
        terms = [terms[i] + terms[i + 1] for i in range(0, len(terms), 2)]
    return terms[0]


def take(x, index):
    return lax.dynamic_index_in_dim(x, index, 0, keepdims=False)


def in_order(parts, index):
    x = jnp.stack(parts)
    n = x.shape[0]
    width = 1
    while width < n:
        y = x.reshape((n // (2 * width), 2, width) + x.shape[1:])
        flipped = jnp.stack([y[:, 1], y[:, 0]], 1)
        x = jnp.where((index & width) != 0, flipped, y).reshape(x.shape)
        width *= 2
    return x


def per_device(observed, first_factor, second_factor, third_factor):
    row_count = lax.axis_size("row")
    col_count = lax.axis_size("col")
    chip_count = row_count // 2
    for n in (chip_count, col_count):
        assert n & (n - 1) == 0
    rows_here, depth_count, cols_here = observed.shape
    rank = third_factor.shape[1]
    rows_own, cols_own = first_factor.shape[0], second_factor.shape[0]
    half_depth = depth_count // 2
    cols_half = cols_here // 2
    row = lax.axis_index("row")
    col = lax.axis_index("col")
    core, chip = row & 1, row >> 1
    rate_one = step_rate / (cols_here * col_count * depth_count)
    rate_two = step_rate / (rows_here * row_count * depth_count)
    rate_three = step_rate / (rows_here * row_count * cols_here * col_count)
    chip_masks = []
    bit = 1
    while bit < chip_count:
        chip_masks.append(bit | (bit >> 1))
        bit *= 2

    def gather_rows(own, sent):
        parts = [own] + [exchange(sent, "col", s) for s in range(1, col_count)]
        return in_order(parts, col).reshape(rows_here, rank)

    def both_cores(half, depth_half):
        other = exchange(jnp.concatenate([half.reshape(cols_half, rank), depth_half]), "row", 1)
        other_half = other[:cols_half].reshape(half.shape)
        other_depth = other[cols_half:]
        wide = jnp.where(core == 0, jnp.stack([half, other_half], 1), jnp.stack([other_half, half], 1))
        depth = jnp.where(core == 0, jnp.concatenate([depth_half, other_depth]),
                          jnp.concatenate([other_depth, depth_half]))
        return wide.reshape(cols_here, rank), depth

    a, b, c = staged(first_factor, second_factor, third_factor)
    head = first_block(observed, 8, 128)
    c_half = lax.dynamic_slice_in_dim(c, core * half_depth, half_depth, 0)
    held = [b]
    places = [0]
    mask = chip_count // 2
    while mask:
        sent = jnp.stack(held) if len(held) > 1 else second_factor[None]
        got = exchange(sent, "row", 2 * mask)
        held = held + [got[i] for i in range(len(held))]
        places = places + [p ^ mask for p in places]
        mask //= 2
    b_half = in_order([held[places.index(s)] for s in range(chip_count)], chip)
    wide_a = gather_rows(a, first_factor)
    wide_b, c = both_cores(b_half, c_half)
    for iteration in range(STEPS):
        last = iteration == STEPS - 1
        ga, keep, send = gradients(observed, head, wide_a, wide_b, c, cols_own)
        ga = ga.reshape(col_count, rows_own, rank)
        both = keep + exchange(send, "row", 1)
        gb, gc = both[:cols_half], both[cols_half:]
        parts = [jnp.concatenate([take(ga, col), gc])]
        for s in range(1, col_count):
            parts.append(exchange(jnp.concatenate([take(ga, col ^ s), gc]), "col", s))
        both = tree_sum(parts)
        a = a - rate_one * both[:rows_own]
        gc = both[rows_own:]
        if last:
            gb = gb.reshape(chip_count, cols_own, rank)
            parts = [jnp.concatenate([take(gb, chip), gc])]
            for s in range(1, chip_count):
                parts.append(exchange(jnp.concatenate([take(gb, chip ^ s), gc]), "row", 2 * s))
            both = tree_sum(parts)
            b = take(b_half, chip) - rate_two * both[:cols_own]
            c_half = c_half - rate_three * both[cols_own:]
            other = exchange(c_half, "row", 1)
            c = jnp.where(core == 0, jnp.concatenate([c_half, other]), jnp.concatenate([other, c_half]))
        else:
            both = jnp.concatenate([gb, gc])
            for mask in chip_masks:
                both = both + exchange(both, "row", 2 * mask)
            wide_a = gather_rows(a, a)
            b_half = b_half - rate_two * both[:cols_half].reshape(b_half.shape)
            c_half = c_half - rate_three * both[cols_half:]
            wide_b, c = both_cores(b_half, c_half)
    return (a, b, c)


def solution(mesh):
    return jax.shard_map(
        per_device,
        mesh=mesh,
        in_specs=(P("row", None, "col"), P(("row", "col"), None), P(("col", "row"), None), P()),
        out_specs=(P(("row", "col"), None), P(("col", "row"), None), P()),
        check_vma=False,
    )
```

```python
import functools

import jax
import jax.numpy as jnp
from jax import lax
from jax.experimental import pallas as pl
from jax.experimental.pallas import tpu as pltpu
from jax.sharding import PartitionSpec as P


STEPS = 2
step_rate = 48.0
f32 = jnp.float32
bf16 = jnp.bfloat16
VMEM_BYTES = 20 * 1024 * 1024


def split(x):
    high = x.astype(bf16)
    low = (x - high.astype(f32)).astype(bf16)
    return high, low


def panel_copy(obs_hbm, dst, sem, block, panel, depth_block):
    lanes = dst.shape[-1]
    return pltpu.make_async_copy(
        obs_hbm.at[:, pl.ds(block * depth_block, depth_block), pl.ds(panel * lanes, lanes)], dst, sem)


def grad_kernel(obs_hbm, head_ref, a_ref, b_ref, c_ref, ga_ref, keep_ref, send_ref,
                obs, bt_cat, b_cat, at_cat, gbt, gb_ref, gc_ref, ahead, sems, *, group, cols_own):
    panels, n, depth_block, lanes = head_ref.shape
    blocks = c_ref.shape[0] // depth_block

    def fetch(g, h):
        return panel_copy(obs_hbm, obs.at[g, h], sems.at[g, h], g + 1, h, depth_block)

    for g in range(blocks - 1):
        for h in range(panels):
            fetch(g, h).start()
    b = b_ref[...]
    bh, bl = split(b)
    b_cat[...] = jnp.concatenate([bh, bl, bh], 0)
    bth, btl = split(0.5 * b.T)
    bt_cat[...] = jnp.concatenate([bth, btl, bth], 0)
    ath, atl = split(a_ref[...].T)
    at_cat[...] = jnp.concatenate([ath, ath, atl], 1)
    ga_ref[...] = jnp.zeros_like(ga_ref)
    gbt[...] = jnp.zeros_like(gbt)

    def front(rows):
        wide = []
        for k in range(group):
            ph, pw = split(a_ref[...] * rows[k:k + 1, :])
            wide.append(jnp.concatenate([ph, ph, pw], 1))
        return jnp.dot(jnp.concatenate(wide, 0), bt_cat[...], preferred_element_type=f32)

    def block(g, source, more=True):
        flat = [source.at[h].reshape(n * depth_block, lanes) for h in range(panels)]
        a = a_ref[...]
        base = pl.multiple_of(g * depth_block, depth_block)
        ck = c_ref[pl.ds(base, depth_block), :]
        ckt = ck.T
        rows_c = []

        if more:
            following = c_ref[pl.ds(pl.multiple_of(base + depth_block, depth_block), depth_block), :]
        later = ahead[...]
        for k0 in range(0, depth_block, group):
            logits = later
            if k0 + group < depth_block:
                later = front(ck[k0 + group:k0 + 2 * group])
            elif more:
                ahead[...] = front(following[:group])
            x = jnp.concatenate([
                jnp.concatenate([p[pl.ds(k, n, stride=depth_block), :] for p in flat], 1)
                for k in range(k0, k0 + group)], 0)
            derivative = 0.5 * jnp.tanh(logits) + (0.5 - x.astype(f32))
            dh, dw = split(derivative)
            carried = jnp.dot(
                jnp.concatenate([dh, dh, dw], 1), b_cat[...], preferred_element_type=f32)
            total = None
            for q in range(group):
                k = k0 + q
                cq = carried[q * n:(q + 1) * n]
                term = cq * ck[k:k + 1, :]
                total = term if total is None else total + term
                rows_c.append(jnp.sum(cq * a, axis=0, keepdims=True))
            ga_ref[...] += total
            total = None
            for q in range(group):
                k = k0 + q
                dhq = dh[q * n:(q + 1) * n]
                dwq = dw[q * n:(q + 1) * n]
                gt = jnp.dot(
                    at_cat[...], jnp.concatenate([dhq, dwq, dhq], 0), preferred_element_type=f32)
                term = gt * ckt[:, k:k + 1]
                total = term if total is None else total + term
            gbt[...] += total
        gc_ref[pl.ds(base, depth_block), :] = jnp.concatenate(rows_c, 0)

    def rest(g, carry):
        for h in range(panels):
            fetch(g, h).wait()
        block(g + 1, obs.at[g])
        return carry

    ahead[...] = front(c_ref[:group, :])
    block(0, head_ref)
    lax.fori_loop(0, blocks - 2, rest, 0)
    for h in range(panels):
        fetch(blocks - 2, h).wait()
    block(blocks - 1, obs.at[blocks - 2], more=False)
    gb_ref[...] = gbt[...].T
    core = lax.axis_index("row") & 1
    half_depth = gc_ref.shape[0] // 2
    half = gb_ref.shape[0] // 2
    for ref, which in ((keep_ref, core), (send_ref, 1 - core)):
        for p in range(half // cols_own):
            start = pl.multiple_of((2 * p + which) * cols_own, cols_own)
            ref[p * cols_own:(p + 1) * cols_own, :] = gb_ref[pl.ds(start, cols_own), :]
        start = pl.multiple_of(which * half_depth, half_depth)
        ref[half:, :] = gc_ref[pl.ds(start, half_depth), :]


def gradients(observed, head, a, b, c, cols_own):
    rows, depth, cols = observed.shape
    rank = a.shape[1]
    panels, _, depth_block, lanes = head.shape
    blocks = depth // depth_block
    group = 2
    here = pl.BlockSpec(memory_space=pltpu.VMEM)
    return pl.pallas_call(
        functools.partial(grad_kernel, group=group, cols_own=cols_own),
        in_specs=[pl.BlockSpec(memory_space=pltpu.HBM), here, here, here, here],
        out_specs=[here, here, here],
        out_shape=[
            jax.ShapeDtypeStruct((rows, rank), f32),
            jax.ShapeDtypeStruct(((cols + depth) // 2, rank), f32),
            jax.ShapeDtypeStruct(((cols + depth) // 2, rank), f32),
        ],
        scratch_shapes=[
            pltpu.VMEM((blocks - 1, panels, rows, depth_block, lanes), jnp.int32),
            pltpu.VMEM((3 * rank, cols), bf16), pltpu.VMEM((3 * cols, rank), bf16),
            pltpu.VMEM((rank, 3 * rows), bf16), pltpu.VMEM((rank, cols), f32),
            pltpu.VMEM((cols, rank), f32), pltpu.VMEM((depth, rank), f32),
            pltpu.VMEM((group * rows, cols), f32),
            pltpu.SemaphoreType.DMA((blocks - 1, panels)),
        ],
        compiler_params=pltpu.CompilerParams(vmem_limit_bytes=VMEM_BYTES),
        cost_estimate=pl.CostEstimate(
            flops=18 * rows * depth * cols * rank, bytes_accessed=4 * rows * depth * cols,
            transcendentals=rows * depth * cols),
    )(pltpu.with_memory_space_constraint(observed, pltpu.HBM), head, a, b, c)


def head_kernel(obs_hbm, head_ref, sems):
    copies = [
        panel_copy(obs_hbm, head_ref.at[h], sems.at[h], 0, h, head_ref.shape[2])
        for h in range(head_ref.shape[0])
    ]
    for copy in copies:
        copy.start()
    for copy in copies:
        copy.wait()


def first_block(observed, depth_block, lanes):
    rows, _, cols = observed.shape
    panels = cols // lanes
    return pl.pallas_call(
        head_kernel,
        in_specs=[pl.BlockSpec(memory_space=pltpu.HBM)],
        out_specs=pl.BlockSpec(memory_space=pltpu.VMEM),
        out_shape=jax.ShapeDtypeStruct((panels, rows, depth_block, lanes), observed.dtype),
        scratch_shapes=[pltpu.SemaphoreType.DMA((panels,))],
        compiler_params=pltpu.CompilerParams(vmem_limit_bytes=VMEM_BYTES),
    )(pltpu.with_memory_space_constraint(observed, pltpu.HBM))


def exchange(x, axis, mask):
    n = lax.axis_size(axis)
    return lax.ppermute(x, axis, [(i, i ^ mask) for i in range(n)])


def stage_kernel(a_hbm, b_hbm, c_hbm, a_ref, b_ref, c_ref, sems):
    copies = [
        pltpu.make_async_copy(src, dst, sems.at[i])
        for i, (src, dst) in enumerate(((a_hbm, a_ref), (b_hbm, b_ref), (c_hbm, c_ref)))
    ]
    for copy in copies:
        copy.start()
    for copy in copies:
        copy.wait()


def staged(a, b, c):
    return pl.pallas_call(
        stage_kernel,
        in_specs=[pl.BlockSpec(memory_space=pltpu.HBM)] * 3,
        out_specs=[pl.BlockSpec(memory_space=pltpu.VMEM)] * 3,
        out_shape=[jax.ShapeDtypeStruct(x.shape, x.dtype) for x in (a, b, c)],
        scratch_shapes=[pltpu.SemaphoreType.DMA((3,))],
        compiler_params=pltpu.CompilerParams(vmem_limit_bytes=VMEM_BYTES),
    )(*[pltpu.with_memory_space_constraint(x, pltpu.HBM) for x in (a, b, c)])


def tree_sum(terms):
    while len(terms) > 1:
        terms = [terms[i] + terms[i + 1] for i in range(0, len(terms), 2)]
    return terms[0]


def take(x, index):
    return lax.dynamic_index_in_dim(x, index, 0, keepdims=False)


def in_order(parts, index):
    x = jnp.stack(parts)
    n = x.shape[0]
    width = 1
    while width < n:
        y = x.reshape((n // (2 * width), 2, width) + x.shape[1:])
        flipped = jnp.stack([y[:, 1], y[:, 0]], 1)
        x = jnp.where((index & width) != 0, flipped, y).reshape(x.shape)
        width *= 2
    return x


def per_device(observed, first_factor, second_factor, third_factor):
    row_count = lax.axis_size("row")
    col_count = lax.axis_size("col")
    chip_count = row_count // 2
    for n in (chip_count, col_count):
        assert n & (n - 1) == 0
    rows_here, depth_count, cols_here = observed.shape
    rank = third_factor.shape[1]
    rows_own, cols_own = first_factor.shape[0], second_factor.shape[0]
    half_depth = depth_count // 2
    cols_half = cols_here // 2
    row = lax.axis_index("row")
    col = lax.axis_index("col")
    core, chip = row & 1, row >> 1
    rate_one = step_rate / (cols_here * col_count * depth_count)
    rate_two = step_rate / (rows_here * row_count * depth_count)
    rate_three = step_rate / (rows_here * row_count * cols_here * col_count)
    chip_masks = []
    bit = 1
    while bit < chip_count:
        chip_masks.append(bit | (bit >> 1))
        bit *= 2

    def gather_rows(own, sent):
        parts = [own] + [exchange(sent, "col", s) for s in range(1, col_count)]
        return in_order(parts, col).reshape(rows_here, rank)

    def both_cores(half, depth_half):
        other = exchange(jnp.concatenate([half.reshape(cols_half, rank), depth_half]), "row", 1)
        other_half = other[:cols_half].reshape(half.shape)
        other_depth = other[cols_half:]
        wide = jnp.where(core == 0, jnp.stack([half, other_half], 1), jnp.stack([other_half, half], 1))
        depth = jnp.where(core == 0, jnp.concatenate([depth_half, other_depth]),
                          jnp.concatenate([other_depth, depth_half]))
        return wide.reshape(cols_here, rank), depth

    a, b, c = staged(first_factor, second_factor, third_factor)
    head = first_block(observed, 8, 128)
    c_half = lax.dynamic_slice_in_dim(c, core * half_depth, half_depth, 0)
    held = [b]
    places = [0]
    mask = chip_count // 2
    while mask:
        sent = jnp.stack(held) if len(held) > 1 else second_factor[None]
        got = exchange(sent, "row", 2 * mask)
        held = held + [got[i] for i in range(len(held))]
        places = places + [p ^ mask for p in places]
        mask //= 2
    b_half = in_order([held[places.index(s)] for s in range(chip_count)], chip)
    wide_a = gather_rows(a, first_factor)
    wide_b, c = both_cores(b_half, c_half)
    for iteration in range(STEPS):
        last = iteration == STEPS - 1
        ga, keep, send = gradients(observed, head, wide_a, wide_b, c, cols_own)
        ga = ga.reshape(col_count, rows_own, rank)
        both = keep + exchange(send, "row", 1)
        gb, gc = both[:cols_half], both[cols_half:]
        parts = [jnp.concatenate([take(ga, col), gc])]
        for s in range(1, col_count):
            parts.append(exchange(jnp.concatenate([take(ga, col ^ s), gc]), "col", s))
        both = tree_sum(parts)
        a = a - rate_one * both[:rows_own]
        gc = both[rows_own:]
        if last:
            gb = gb.reshape(chip_count, cols_own, rank)
            parts = [jnp.concatenate([take(gb, chip), gc])]
            for s in range(1, chip_count):
                parts.append(exchange(jnp.concatenate([take(gb, chip ^ s), gc]), "row", 2 * s))
            both = tree_sum(parts)
            b = take(b_half, chip) - rate_two * both[:cols_own]
            c_half = c_half - rate_three * both[cols_own:]
            other = exchange(c_half, "row", 1)
            c = jnp.where(core == 0, jnp.concatenate([c_half, other]), jnp.concatenate([other, c_half]))
        else:
            both = jnp.concatenate([gb, gc])
            for mask in chip_masks:
                both = both + exchange(both, "row", 2 * mask)
            wide_a = gather_rows(a, a)
            b_half = b_half - rate_two * both[:cols_half].reshape(b_half.shape)
            c_half = c_half - rate_three * both[cols_half:]
            wide_b, c = both_cores(b_half, c_half)
    return (a, b, c)


def solution(mesh):
    return jax.shard_map(
        per_device,
        mesh=mesh,
        in_specs=(P("row", None, "col"), P(("row", "col"), None), P(("col", "row"), None), P()),
        out_specs=(P(("row", "col"), None), P(("col", "row"), None), P()),
        check_vma=False,
    )
```
